256 devices in a mesh: row: 16 (over z, x_hi), col: 16 (over x_lo, y, core).
Axes of the slice: x: 4 (x_hi: 2, x_lo: 2; x = x_hi * 2 + x_lo), y: 4, z: 8, core: 2. Of those that a mesh axis runs over, the one named last changes fastest.
Arguments:
- features: bfloat16 [96, 256, 4096], P(None, 'row', 'col'), may hold values from -6 to 6
- teacher: bfloat16 [1536, 256, 4096], P(None, 'row', 'col'), may hold values from -6 to 6
- conv_in: bfloat16 [9, 96, 96], replicated, may hold values from -0.21875 to 0.21875
- conv_out: bfloat16 [9, 96, 96], replicated, may hold values from -0.21875 to 0.21875
- projector: bfloat16 [96, 1536], replicated, may hold values from -0.625 to 0.625
Outputs:
- grad_conv_in: float32 [9, 96, 96], replicated
- grad_conv_out: float32 [9, 96, 96], replicated
- grad_projector: float32 [96, 1536], replicated
The draws below stay inside these ranges and needn't reach their ends.
All inputs are finite; a program needn't handle non-finite values.
Results may differ from the reference program's by a relative error of at most 0.0003.
Values may be sent and summed in bfloat16 or wider, within the bound.
A program may use at most 128 MiB of HBM per device.

```python
import jax
import jax.numpy as jnp
from jax import lax

C = 96
E = 1536
TH = 16
IMG_H = 256
IMG_W = 4096


def block_scale(key, extent, shards, low, high):
    loudness = 1.0
    for position, parts in shards:
        draws = jax.random.uniform(jax.random.fold_in(jax.random.fold_in(key, 6), position), (parts,), jnp.float32, low / len(shards), high / len(shards))
        loudness = loudness * jnp.repeat(jnp.exp(draws), extent[position] // parts).reshape((-1,) + (1,) * (len(extent) - 1 - position))
    return loudness


def scatter_about(rng, shape, scale, limit, cuts=(), held_as=jnp.bfloat16):
    drawn = scale * jax.random.normal(rng, shape, jnp.float32)
    if cuts:
        drawn = drawn * block_scale(rng, shape, cuts, -0.22, 0.18)
    return jnp.clip(drawn, -limit, limit).astype(held_as)


def setup_inputs(seed: int = 0) -> dict:
    keys = jax.random.split(jax.random.key(seed), 6)
    features = scatter_about(keys[0], (C, IMG_H, IMG_W), 1.0, 6.0, ((1, 16), (2, 16)))
    teacher = scatter_about(keys[1], (E, IMG_H, IMG_W), 1.0, 6.0, ((1, 16), (2, 16)))
    conv_in = scatter_about(keys[2], (9, C, C), (9 * C) ** -0.5, 0.21875)
    conv_out = scatter_about(keys[3], (9, C, C), (9 * C) ** -0.5, 0.21875)
    projector = scatter_about(keys[4], (C, E), C ** -0.5, 0.625)
    return dict(features=features, teacher=teacher, conv_in=conv_in, conv_out=conv_out, projector=projector)


def gelu_grad(value):
    cdf = 0.5 * (1.0 + jax.scipy.special.erf(value * 0.7071067811865476))
    dens = jnp.exp(-0.5 * value * value) * 0.3989422804014327
    return cdf + value * dens

def padded_field(field):
    return jnp.pad(field.astype(jnp.float32), ((0, 0), (1, 1), (1, 1)))

def conv_full(padded, kernel):
    total = jnp.zeros((kernel.shape[2], IMG_H, IMG_W), jnp.float32)
    for tap in range(9):
        shift_a, shift_b = (tap // 3, tap % 3)
        window = padded[:, shift_a:shift_a + IMG_H, shift_b:shift_b + IMG_W]
        total = total + jnp.einsum('co,chw->ohw', kernel[tap].astype(jnp.float32), window)
    return total

def reference(features, teacher, conv_in, conv_out, projector):
    xpad = padded_field(features)
    pre = conv_full(xpad, conv_in)
    hidden = jax.nn.gelu(pre, approximate=False).astype(jnp.bfloat16)
    gpad = padded_field(hidden)
    student = (features.astype(jnp.float32) + conv_full(gpad, conv_out)).astype(jnp.bfloat16)
    npix = IMG_H * IMG_W
    proj_f = projector.astype(jnp.float32)
    blocks = IMG_H // TH

    def one_block(carry, index):
        start = (index * TH).astype(jnp.int32)
        stud = lax.dynamic_slice_in_dim(student, start, TH, 1).astype(jnp.float32)
        teach = lax.dynamic_slice_in_dim(teacher, start, TH, 1).astype(jnp.float32)
        pred = jnp.einsum('ce,chw->ehw', proj_f, stud)
        dpred = ((pred - teach) / npix).astype(jnp.bfloat16).astype(jnp.float32)
        carry = carry + jnp.einsum('chw,ehw->ce', stud, dpred)
        dstud = jnp.einsum('ce,ehw->chw', proj_f, dpred).astype(jnp.bfloat16)
        return (carry, dstud)
    grad_projector, pieces = lax.scan(one_block, jnp.zeros((C, E), jnp.float32), jnp.arange(blocks, dtype=jnp.int32))
    dstudent = jnp.transpose(pieces, (1, 0, 2, 3)).reshape(C, IMG_H, IMG_W)
    spad = padded_field(dstudent)
    dhidden = jnp.zeros((C, IMG_H, IMG_W), jnp.float32)
    for tap in range(9):
        shift_a, shift_b = (tap // 3, tap % 3)
        window = spad[:, 2 - shift_a:2 - shift_a + IMG_H, 2 - shift_b:2 - shift_b + IMG_W]
        dhidden = dhidden + jnp.einsum('co,ohw->chw', conv_out[tap].astype(jnp.float32), window)
    dpre = (dhidden * gelu_grad(pre)).astype(jnp.bfloat16).astype(jnp.float32)
    dstud_f = dstudent.astype(jnp.float32)
    grad_out_list = []
    grad_in_list = []
    for tap in range(9):
        shift_a, shift_b = (tap // 3, tap % 3)
        gwin = gpad[:, shift_a:shift_a + IMG_H, shift_b:shift_b + IMG_W]
        xwin = xpad[:, shift_a:shift_a + IMG_H, shift_b:shift_b + IMG_W]
        grad_out_list.append(jnp.einsum('chw,ohw->co', gwin, dstud_f))
        grad_in_list.append(jnp.einsum('chw,ohw->co', xwin, dpre))
    return (jnp.stack(grad_in_list), jnp.stack(grad_out_list), grad_projector)
```

```python
import functools

import jax
import jax.numpy as jnp
from jax import lax
from jax.experimental import pallas as pl
from jax.experimental.pallas import tpu as pltpu
from jax.sharding import PartitionSpec as P

MESH = pl.DeviceIdType.MESH
ROWS = 3072
HALF = 1536
COLOUR = 768
BIG = 192
SMALL = 48


def place():
    row, col = lax.axis_index("row"), lax.axis_index("col")
    return dict(
        x=(row % 2) * 2 + col // 8, y=(col // 2) % 4, z=row // 2, core=col % 2
    )


def device(at, **moved):
    p = dict(at, **moved)
    return (p["z"] * 2 + p["x"] // 2, ((p["x"] % 2) * 4 + p["y"]) * 2 + p["core"])


def peers(at):
    yield device(at, core=1 - at["core"])
    for axis, n in (("x", 4), ("y", 4), ("z", 8)):
        for step in range(1, n):
            yield device(at, **{axis: (at[axis] + step) % n})


def reduce_kernel(v, gin, gout, gproj, r, w, in0, in1, in2, out3, in3, sums3, sent, got):
    at = place()
    barrier = pltpu.get_barrier_semaphore()
    for peer in peers(at):
        pl.semaphore_signal(barrier, inc=1, device_id=peer, device_id_type=MESH)
    pl.semaphore_wait(barrier, 14)

    number = iter(range(100))

    def copy(src, dst, peer):
        k = next(number)
        c = pltpu.make_async_remote_copy(
            src_ref=src,
            dst_ref=dst,
            send_sem=sent.at[k],
            recv_sem=got.at[k],
            device_id=peer,
            device_id_type=MESH,
        )
        c.start()
        return c

    def al(x, m):
        return pl.multiple_of(x, m)

    started = []
    core = at["core"]
    c = copy(v.at[pl.ds(al((1 - core) * HALF, 8), HALF)], in0, device(at, core=1 - core))
    started.append(c)
    c.wait_recv()
    mine = al(core * HALF, 8)
    w[...] = v[pl.ds(mine, HALF)] + in0[...]

    orders = (("x", "y"), ("y", "x"))
    starts = []
    waits = []
    for colour, (first, second) in enumerate(orders):
        base = colour * COLOUR
        row = []
        for step in range(1, 4):
            q = (at[first] + step) % 4
            row.append(
                copy(
                    w.at[pl.ds(al(base + q * BIG, 8), BIG)],
                    in1.at[colour, step - 1],
                    device(at, **{first: q}),
                )
            )
        waits.append(row)
    for colour, (first, second) in enumerate(orders):
        for c in waits[colour]:
            c.wait_recv()
        start = al(colour * COLOUR + at[first] * BIG, 8)
        w[pl.ds(start, BIG)] = (
            w[pl.ds(start, BIG)] + in1[colour, 0] + in1[colour, 1] + in1[colour, 2]
        )
        starts.append(start)
        started += waits[colour]
    waits = []
    for colour, (first, second) in enumerate(orders):
        row = []
        for step in range(1, 4):
            q = (at[second] + step) % 4
            row.append(
                copy(
                    w.at[pl.ds(al(starts[colour] + q * SMALL, 8), SMALL)],
                    in2.at[colour, step - 1],
                    device(at, **{second: q}),
                )
            )
        waits.append(row)
    smalls = []
    for colour, (first, second) in enumerate(orders):
        for c in waits[colour]:
            c.wait_recv()
        start = al(starts[colour] + at[second] * SMALL, 8)
        total = w[pl.ds(start, SMALL)] + in2[colour, 0] + in2[colour, 1] + in2[colour, 2]
        out3[pl.ds(colour * 12, 12)] = total.reshape(12, 4, 128)
        smalls.append(start)
        started += waits[colour]
    z = at["z"]
    row = []
    for step in range(1, 8):
        q = (z + step) % 8
        row.append(copy(out3.at[pl.ds(q * 3, 3)], in3.at[step - 1], device(at, z=q)))
    for c in row:
        c.wait_recv()
    started += row
    total = out3[pl.ds(z * 3, 3)]
    for k in range(7):
        total = total + in3[k]
    sums3[pl.ds(z * 3, 3)] = total
    row = []
    for step in range(1, 8):
        q = (z + step) % 8
        row.append(
            copy(sums3.at[pl.ds(z * 3, 3)], sums3.at[pl.ds(z * 3, 3)], device(at, z=q))
        )
    for c in row:
        c.wait_recv()
    started += row
    waits = []
    for colour, (first, second) in enumerate(orders):
        rows = pl.ds(al(mine + smalls[colour], 8), SMALL)
        r[rows] = sums3[pl.ds(colour * 12, 12)].reshape(SMALL, 128)
        for step in range(1, 4):
            q = (at[second] + step) % 4
            waits.append(copy(r.at[rows], r.at[rows], device(at, **{second: q})))
    for c in waits:
        c.wait_recv()
    started += waits
    waits = []
    other = device(at, core=1 - core)
    last = []
    for colour, (first, second) in enumerate(orders):
        rows = pl.ds(al(mine + starts[colour], 8), BIG)
        for step in range(1, 4):
            q = (at[first] + step) % 4
            waits.append(copy(r.at[rows], r.at[rows], device(at, **{first: q})))
        last.append(copy(r.at[rows], r.at[rows], other))
    k = 0
    for colour, (first, second) in enumerate(orders):
        for step in range(1, 4):
            q = (at[first] - step + 4) % 4
            rows = pl.ds(al(mine + colour * COLOUR + q * BIG, 8), BIG)
            waits[k].wait_recv()
            last.append(copy(r.at[rows], r.at[rows], other))
            k += 1
    for c in last:
        c.wait_recv()
    started += waits + last
    for c in started:
        c.wait_send()
    for t in range(9):
        gin[t] = r[t * 96 : (t + 1) * 96, :96]
        gout[t] = r[864 + t * 96 : 864 + (t + 1) * 96, :96]
    for t in range(12):
        gproj[:, t * 128 : (t + 1) * 128] = r[1728 + t * 96 : 1728 + (t + 1) * 96]


def all_reduce(v):
    f32 = jnp.float32
    vmem = pl.BlockSpec(memory_space=pltpu.VMEM)
    return pl.pallas_call(
        reduce_kernel,
        out_shape=(
            jax.ShapeDtypeStruct((9, 96, 96), f32),
            jax.ShapeDtypeStruct((9, 96, 96), f32),
            jax.ShapeDtypeStruct((96, 1536), f32),
        ),
        in_specs=[vmem],
        out_specs=(vmem, vmem, vmem),
        scratch_shapes=[
            pltpu.VMEM((ROWS, 128), f32),
            pltpu.VMEM((HALF, 128), f32),
            pltpu.VMEM((HALF, 128), f32),
            pltpu.VMEM((2, 3, BIG, 128), f32),
            pltpu.VMEM((2, 3, SMALL, 128), f32),
            pltpu.VMEM((24, 4, 128), f32),
            pltpu.VMEM((7, 3, 4, 128), f32),
            pltpu.VMEM((24, 4, 128), f32),
            pltpu.SemaphoreType.DMA((48,)),
            pltpu.SemaphoreType.DMA((48,)),
        ],
        compiler_params=pltpu.CompilerParams(
            collective_id=1, has_side_effects=True, vmem_limit_bytes=40 * 2**20
        ),
    )(v)


def padded_2(cells, sides, width):
    for axis, dim in sides:
        count = lax.axis_size(axis)
        ends = count - 1
        head = lax.slice_in_dim(cells, 0, width, axis=dim)
        tail = lax.slice_in_dim(cells, cells.shape[dim] - width, cells.shape[dim], axis=dim)
        cells = jnp.concatenate(
            [
                lax.ppermute(tail, axis, [(i, (i + 1) % count) for i in range(ends)]),
                cells,
                lax.ppermute(head, axis, [((i + 1) % count, i) for i in range(ends)]),
            ],
            axis=dim,
        )
    return cells


def gelu_grad(value):
    cdf = 0.5 * (1.0 + jax.scipy.special.erf(value * 0.7071067811865476))
    dens = jnp.exp(-0.5 * value * value) * 0.3989422804014327
    return cdf + value * dens


def tap_stack(padded, height, width):
    return jnp.concatenate(
        [padded[:, tap // 3 : tap // 3 + height, tap % 3 : tap % 3 + width] for tap in range(9)], 0
    )


def flip_stack(padded, height, width):
    return jnp.concatenate(
        [
            padded[:, 2 - tap // 3 : 2 - tap // 3 + height, 2 - tap % 3 : 2 - tap % 3 + width]
            for tap in range(9)
        ],
        0,
    )


def shards(features, teacher, conv_in, conv_out, projector):
    chans, height, width = features.shape
    flat_in = conv_in.reshape(9 * chans, chans)
    flat_out = conv_out.reshape(9 * chans, chans)
    xpad = padded_2(features, (("row", 1), ("col", 2)), 1)
    x_taps = tap_stack(xpad, height, width)
    pre = jnp.einsum("ko,khw->ohw", flat_in, x_taps, preferred_element_type=jnp.float32)
    hidden = jax.nn.gelu(pre, approximate=False).astype(jnp.bfloat16)
    gpad = padded_2(hidden, (("row", 1), ("col", 2)), 1)
    g_taps = tap_stack(gpad, height, width)
    branch = jnp.einsum("ko,khw->ohw", flat_out, g_taps, preferred_element_type=jnp.float32)
    student = (features.astype(jnp.float32) + branch).astype(jnp.bfloat16)
    pred = jnp.einsum("ce,chw->ehw", projector, student, preferred_element_type=jnp.float32)
    npix = height * width * lax.axis_size("row") * lax.axis_size("col")
    dpred = ((pred - teacher.astype(jnp.float32)) / npix).astype(jnp.bfloat16)
    grad_proj = jnp.einsum("chw,ehw->ce", student, dpred, preferred_element_type=jnp.float32)
    dstudent = jnp.einsum(
        "ce,ehw->chw", projector, dpred, preferred_element_type=jnp.float32
    ).astype(jnp.bfloat16)
    spad = padded_2(dstudent, (("row", 1), ("col", 2)), 1)
    back_matrix = jnp.transpose(conv_out, (0, 2, 1)).reshape(9 * chans, chans)
    dhidden = jnp.einsum(
        "kc,khw->chw",
        back_matrix,
        flip_stack(spad, height, width),
        preferred_element_type=jnp.float32,
    )
    dpre = (dhidden * gelu_grad(pre)).astype(jnp.bfloat16)
    grad_out = jnp.einsum(
        "khw,ohw->ko", g_taps, dstudent, preferred_element_type=jnp.float32
    ).reshape(9, chans, chans)
    grad_in = jnp.einsum("khw,ohw->ko", x_taps, dpre, preferred_element_type=jnp.float32).reshape(
        9, chans, chans
    )
    flat = jnp.concatenate(
        [
            jnp.pad(grad_in.reshape(864, 96), ((0, 0), (0, 32))),
            jnp.pad(grad_out.reshape(864, 96), ((0, 0), (0, 32))),
            grad_proj.reshape(96, 12, 128).transpose(1, 0, 2).reshape(1152, 128),
            jnp.zeros((192, 128), jnp.float32),
        ]
    )
    return all_reduce(flat)


def solution(mesh):
    in_specs = (P(None, "row", "col"), P(None, "row", "col"), P(), P(), P())
    out_specs = (P(), P(), P())
    return jax.shard_map(shards, mesh=mesh, in_specs=in_specs, out_specs=out_specs, check_vma=False)
```

```python
import functools

import jax
import jax.numpy as jnp
from jax import lax
from jax.experimental import pallas as pl
from jax.experimental.pallas import tpu as pltpu
from jax.sharding import PartitionSpec as P

MESH = pl.DeviceIdType.MESH
ROWS = 3072
HALF = 1536
COLOUR = 768
BIG = 192
SMALL = 48


def place():
    row, col = lax.axis_index("row"), lax.axis_index("col")
    return dict(
        x=(row % 2) * 2 + col // 8, y=(col // 2) % 4, z=row // 2, core=col % 2
    )


def device(at, **moved):
    p = dict(at, **moved)
    return (p["z"] * 2 + p["x"] // 2, ((p["x"] % 2) * 4 + p["y"]) * 2 + p["core"])


def peers(at):
    yield device(at, core=1 - at["core"])
    for axis, n in (("x", 4), ("y", 4), ("z", 8)):
        for step in range(1, n):
            yield device(at, **{axis: (at[axis] + step) % n})


def reduce_kernel(v, gin, gout, gproj, r, w, in0, in1, in2, out3, in3, sums3, sent, got):
    at = place()
    barrier = pltpu.get_barrier_semaphore()
    for peer in peers(at):
        pl.semaphore_signal(barrier, inc=1, device_id=peer, device_id_type=MESH)
    pl.semaphore_wait(barrier, 14)

    number = iter(range(100))

    def copy(src, dst, peer):
        k = next(number)
        c = pltpu.make_async_remote_copy(
            src_ref=src,
            dst_ref=dst,
            send_sem=sent.at[k],
            recv_sem=got.at[k],
            device_id=peer,
            device_id_type=MESH,
        )
        c.start()
        return c

    def al(x, m):
        return pl.multiple_of(x, m)

    started = []
    core = at["core"]
    c = copy(v.at[pl.ds(al((1 - core) * HALF, 8), HALF)], in0, device(at, core=1 - core))
    started.append(c)
    c.wait_recv()
    mine = al(core * HALF, 8)
    w[...] = v[pl.ds(mine, HALF)] + in0[...]

    orders = (("x", "y"), ("y", "x"))
    starts = []
    waits = []
    for colour, (first, second) in enumerate(orders):
        base = colour * COLOUR
        row = []
        for step in range(1, 4):
            q = (at[first] + step) % 4
            row.append(
                copy(
                    w.at[pl.ds(al(base + q * BIG, 8), BIG)],
                    in1.at[colour, step - 1],
                    device(at, **{first: q}),
                )
            )
        waits.append(row)
    for colour, (first, second) in enumerate(orders):
        for c in waits[colour]:
            c.wait_recv()
        start = al(colour * COLOUR + at[first] * BIG, 8)
        w[pl.ds(start, BIG)] = (
            w[pl.ds(start, BIG)] + in1[colour, 0] + in1[colour, 1] + in1[colour, 2]
        )
        starts.append(start)
        started += waits[colour]
    waits = []
    for colour, (first, second) in enumerate(orders):
        row = []
        for step in range(1, 4):
            q = (at[second] + step) % 4
            row.append(
                copy(
                    w.at[pl.ds(al(starts[colour] + q * SMALL, 8), SMALL)],
                    in2.at[colour, step - 1],
                    device(at, **{second: q}),
                )
            )
        waits.append(row)
    smalls = []
    for colour, (first, second) in enumerate(orders):
        for c in waits[colour]:
            c.wait_recv()
        start = al(starts[colour] + at[second] * SMALL, 8)
        total = w[pl.ds(start, SMALL)] + in2[colour, 0] + in2[colour, 1] + in2[colour, 2]
        out3[pl.ds(colour * 12, 12)] = total.reshape(12, 4, 128)
        smalls.append(start)
        started += waits[colour]
    z = at["z"]
    row = []
    for step in range(1, 8):
        q = (z + step) % 8
        row.append(copy(out3.at[pl.ds(q * 3, 3)], in3.at[step - 1], device(at, z=q)))
    for c in row:
        c.wait_recv()
    started += row
    total = out3[pl.ds(z * 3, 3)]
    for k in range(7):
        total = total + in3[k]
    sums3[pl.ds(z * 3, 3)] = total
    row = []
    for step in range(1, 8):
        q = (z + step) % 8
        row.append(
            copy(sums3.at[pl.ds(z * 3, 3)], sums3.at[pl.ds(z * 3, 3)], device(at, z=q))
        )
    for c in row:
        c.wait_recv()
    started += row
    waits = []
    for colour, (first, second) in enumerate(orders):
        rows = pl.ds(al(mine + smalls[colour], 8), SMALL)
        r[rows] = sums3[pl.ds(colour * 12, 12)].reshape(SMALL, 128)
        for step in range(1, 4):
            q = (at[second] + step) % 4
            waits.append(copy(r.at[rows], r.at[rows], device(at, **{second: q})))
    for c in waits:
        c.wait_recv()
    started += waits
    waits = []
    other = device(at, core=1 - core)
    last = []
    for colour, (first, second) in enumerate(orders):
        rows = pl.ds(al(mine + starts[colour], 8), BIG)
        for step in range(1, 4):
            q = (at[first] + step) % 4
            waits.append(copy(r.at[rows], r.at[rows], device(at, **{first: q})))
        last.append(copy(r.at[rows], r.at[rows], other))
    k = 0
    for colour, (first, second) in enumerate(orders):
        for step in range(1, 4):
            q = (at[first] - step + 4) % 4
            rows = pl.ds(al(mine + colour * COLOUR + q * BIG, 8), BIG)
            waits[k].wait_recv()
            last.append(copy(r.at[rows], r.at[rows], other))
            k += 1
    for c in last:
        c.wait_recv()
    started += waits + last
    for c in started:
        c.wait_send()
    for t in range(9):
        gin[t] = r[t * 96 : (t + 1) * 96, :96]
        gout[t] = r[864 + t * 96 : 864 + (t + 1) * 96, :96]
    for t in range(12):
        gproj[:, t * 128 : (t + 1) * 128] = r[1728 + t * 96 : 1728 + (t + 1) * 96]


def all_reduce(v):
    f32 = jnp.float32
    vmem = pl.BlockSpec(memory_space=pltpu.VMEM)
    return pl.pallas_call(
        reduce_kernel,
        out_shape=(
            jax.ShapeDtypeStruct((9, 96, 96), f32),
            jax.ShapeDtypeStruct((9, 96, 96), f32),
            jax.ShapeDtypeStruct((96, 1536), f32),
        ),
        in_specs=[vmem],
        out_specs=(vmem, vmem, vmem),
        scratch_shapes=[
            pltpu.VMEM((ROWS, 128), f32),
            pltpu.VMEM((HALF, 128), f32),
            pltpu.VMEM((HALF, 128), f32),
            pltpu.VMEM((2, 3, BIG, 128), f32),
            pltpu.VMEM((2, 3, SMALL, 128), f32),
            pltpu.VMEM((24, 4, 128), f32),
            pltpu.VMEM((7, 3, 4, 128), f32),
            pltpu.VMEM((24, 4, 128), f32),
            pltpu.SemaphoreType.DMA((48,)),
            pltpu.SemaphoreType.DMA((48,)),
        ],
        compiler_params=pltpu.CompilerParams(
            collective_id=1, has_side_effects=True, vmem_limit_bytes=40 * 2**20
        ),
    )(v)
AROUND = ((-1, 0), (1, 0), (0, -1), (0, 1), (-1, -1), (-1, 1), (1, -1), (1, 1))
SCALE = 2.0**-20
CHUNK = 256


def dot(a, b):
    return jnp.dot(a, b, preferred_element_type=jnp.float32)


def dot_nt(a, b):
    return lax.dot_general(a, b, (((1,), (1,)), ((), ())), preferred_element_type=jnp.float32)


def pieces(value):
    out = []
    for _ in range(3):
        out.append(value.astype(jnp.bfloat16))
        value = value - out[-1].astype(jnp.float32)
    return out


def phi(value):
    return 0.5 * (1.0 + lax.erf(value * 0.7071067811865476))


def main_kernel(
    feat, teach, w1, w2, wb, proj, v,
    fv, tin, t2, xh, hh, gp, ds, lhs, gacc, taps, tile, around, local, sent, got,
):
    bf16, f32 = jnp.bfloat16, jnp.float32
    rows, cols = lax.axis_size("row"), lax.axis_size("col")
    row, col = lax.axis_index("row"), lax.axis_index("col")
    up, down, left, right = row > 0, row < rows - 1, col > 0, col < cols - 1

    def neighbour(dr, dc):
        return ((row + dr + rows) % rows, (col + dc + cols) % cols)

    feat_copy = pltpu.make_async_copy(feat, fv, local.at[0])
    feat_copy.start()
    t_copies = []
    for k in range(1536 // CHUNK):
        part = pl.ds(k * CHUNK, CHUNK)
        t_copies.append(pltpu.make_async_copy(teach.at[part], tin.at[part], local.at[k + 1]))
        t_copies[-1].start()
    barrier = pltpu.get_barrier_semaphore()
    for dr, dc in AROUND:
        pl.semaphore_signal(barrier, inc=1, device_id=neighbour(dr, dc), device_id_type=MESH)

    lane = lax.broadcasted_iota(jnp.int32, (96, 128), 1)
    hpos = (lane * 43) >> 8
    jpos = lane - hpos * 6

    def own_tile(read):
        def step(h, acc):
            x = read(h).astype(f32)
            at = (h + 2) * 6
            hi = pltpu.roll(x[:, 128:], at + 2, 1)
            lo = pltpu.roll(x[:, :128], at + 4, 1)
            here = hpos == h + 2
            acc = jnp.where(here & (jpos < 2), hi, acc)
            return jnp.where(here & (jpos > 3), lo, acc)

        return lax.fori_loop(0, 16, step, jnp.zeros((96, 128), f32))

    def exchange(part, top, bottom, to_top, to_bottom):
        copies = []

        def send(k, src, dst, dr, dc):
            c = pltpu.make_async_remote_copy(
                src_ref=src,
                dst_ref=dst,
                send_sem=sent.at[part, k],
                recv_sem=got.at[part, k],
                device_id=neighbour(dr, dc),
                device_id_type=MESH,
            )
            c.start()
            copies.append(c)

        send(8, top, to_bottom, -1, 0)
        send(9, bottom, to_top, 1, 0)
        for k, (dr, dc) in enumerate(AROUND):
            send(k, tile.at[part], around.at[part, AROUND.index((-dr, -dc))], dr, dc)
        return copies

    def rim(part):
        def get(dr, dc):
            if (dr, dc) == (0, 0):
                return tile[part].astype(f32)
            return around[part, AROUND.index((dr, dc))].astype(f32)

        def band(dr):
            mid = get(dr, 0)
            inner = jnp.where(jpos == 2, pltpu.roll(mid, 126, 1), pltpu.roll(mid, 2, 1))
            outer = jnp.where(jpos < 2, get(dr, -1), get(dr, 1))
            return jnp.where((jpos == 2) | (jpos == 3), inner, outer)

        full = jnp.where(
            hpos < 2,
            pltpu.roll(band(-1), 32, 1),
            jnp.where(hpos < 18, band(0), pltpu.roll(band(1), 96, 1)),
        )
        off = ((jpos < 2) & jnp.logical_not(left)) | ((jpos > 3) & jnp.logical_not(right))
        off = off | ((hpos < 2) & jnp.logical_not(up)) | ((hpos > 17) & jnp.logical_not(down))
        return jnp.where(off, 0.0, full)

    def shifted(buf, count, ahead, edge):
        def step(h, _):
            x = buf[h, 1].astype(f32)
            at = (h + ahead) * 6
            before = pltpu.roll(x, 1, 1)
            first = pltpu.roll(edge, 127 - at, 1)
            buf[h, 0, :, :128] = jnp.where(lane == 0, first, before[:, :128]).astype(bf16)
            buf[h, 0, :, 128:] = before[:, 128:].astype(bf16)
            after = pltpu.roll(x, 255, 1)
            last = pltpu.roll(edge, 123 - at, 1)
            buf[h, 2, :, :128] = after[:, :128].astype(bf16)
            buf[h, 2, :, 128:] = jnp.where(lane == 127, last, after[:, 128:]).astype(bf16)
            return 0

        lax.fori_loop(0, count, step, 0)

    def window(buf, h):
        return buf[pl.ds(h, 3)].reshape(864, 256)

    feat_copy.wait()

    def features(i, _):
        at = pl.multiple_of(i * 16, 16)
        xh[2:18, 1, pl.ds(at, 16), :] = jnp.swapaxes(fv[pl.ds(at, 16)], 0, 1)
        return 0

    lax.fori_loop(0, 6, features, 0)
    tile[0] = own_tile(lambda h: xh[h + 2, 1]).astype(bf16)
    pl.semaphore_wait(barrier, 8)
    first = exchange(0, xh.at[2:4, 1], xh.at[16:18, 1], xh.at[0:2, 1], xh.at[18:20, 1])

    def relayout(i, _):
        at = pl.multiple_of(i * 16, 16)
        t2[:, pl.ds(at, 16), :] = jnp.swapaxes(tin[pl.ds(at, 16)], 0, 1)
        return 0

    for k, c in enumerate(t_copies):
        c.wait()
        lax.fori_loop(k * (CHUNK // 16), (k + 1) * (CHUNK // 16), relayout, 0)
    p = proj[...]
    lhs[...] = jnp.concatenate([-p] + pieces(dot_nt(p, p)), axis=1)
    v[...] = jnp.zeros_like(v)
    gacc[...] = jnp.zeros_like(gacc)

    for c in first:
        c.wait_recv()

    @pl.when(jnp.logical_not(up))
    def _():
        xh[0:2, 1] = jnp.zeros((2, 96, 256), bf16)

    @pl.when(jnp.logical_not(down))
    def _():
        xh[18:20, 1] = jnp.zeros((2, 96, 256), bf16)

    edge = rim(0)
    shifted(xh, 20, 0, edge)

    for t in range(9):
        away = (t // 3 - 1) * 6 + t % 3 - 1
        taps[t * 96 : (t + 1) * 96] = pltpu.roll(edge, (128 - away) % 128, 1).astype(bf16)
    pre = dot(w1[...], taps[...])
    side = (pre * phi(pre)).astype(bf16).astype(f32)
    off = ((jpos < 2) & jnp.logical_not(left)) | ((jpos > 3) & jnp.logical_not(right))
    off = off | ((hpos < 2) & jnp.logical_not(up)) | ((hpos > 17) & jnp.logical_not(down))
    side = jnp.where(off, 0.0, side)

    def conv1(r, _):
        pre = dot(w1[...], window(xh, r))
        cdf = phi(pre)
        gp[r] = cdf + pre * (jnp.exp(-0.5 * pre * pre) * 0.3989422804014327)
        outside = ((r == 0) & jnp.logical_not(up)) | ((r == 17) & jnp.logical_not(down))
        hh[r, 1] = jnp.where(outside, 0.0, pre * cdf).astype(bf16)
        return 0

    lax.fori_loop(0, 18, conv1, 0)
    shifted(hh, 18, 1, side)

    def conv2(h, _):
        s = (xh[h + 2, 1].astype(f32) + dot(w2[...], window(hh, h))).astype(bf16)
        for k in range(3):
            t2[h, 1536 + k * 96 : 1632 + k * 96] = s
        ds[h + 1, 1] = (dot(lhs[...], t2[h]) * SCALE).astype(bf16)
        return 0

    lax.fori_loop(0, 16, conv2, 0)
    tile[1] = own_tile(lambda h: ds[h + 1, 1]).astype(bf16)
    second = exchange(1, ds.at[1, 1], ds.at[16, 1], ds.at[0, 1], ds.at[17, 1])

    def grads(h, _):
        gacc[:, :1632] += dot_nt(t2[h, 1536:1632], t2[h, :1632])
        v[864:1728, :96] += dot_nt(window(hh, h), ds[h + 1, 1])
        return 0

    lax.fori_loop(0, 16, grads, 0)
    mp = sum(dot(m, p) for m in pieces(gacc[:, 1536:1632]))
    gp_out = (mp - gacc[:, :1536]) * SCALE
    for k in range(12):
        v[1728 + k * 96 : 1824 + k * 96] = gp_out[:, k * 128 : (k + 1) * 128]

    for c in second:
        c.wait_recv()

    @pl.when(jnp.logical_not(up))
    def _():
        ds[0, 1] = jnp.zeros((96, 256), bf16)

    @pl.when(jnp.logical_not(down))
    def _():
        ds[17, 1] = jnp.zeros((96, 256), bf16)

    shifted(ds, 18, 1, rim(1))

    def back(h, _):
        dpre = (dot(wb[...], window(ds, h)) * gp[h + 1]).astype(bf16)
        v[:864, :96] += dot_nt(window(xh, h + 1), dpre)
        return 0

    lax.fori_loop(0, 16, back, 0)
    for c in first + second:
        c.wait_send()


def gradients(features, teacher, conv_in, conv_out, projector):
    bf16, f32 = jnp.bfloat16, jnp.float32
    w1 = conv_in.reshape(864, 96).T
    w2 = conv_out.reshape(864, 96).T
    wb = conv_out[::-1].transpose(1, 0, 2).reshape(96, 864)
    vmem = pl.BlockSpec(memory_space=pltpu.VMEM)
    hbm = pl.BlockSpec(memory_space=pl.ANY)
    return pl.pallas_call(
        main_kernel,
        out_shape=jax.ShapeDtypeStruct((ROWS, 128), f32),
        in_specs=[hbm, hbm, vmem, vmem, vmem, vmem],
        out_specs=vmem,
        scratch_shapes=[
            pltpu.VMEM((96, 16, 256), bf16),
            pltpu.VMEM((1536, 16, 256), bf16),
            pltpu.VMEM((16, 1824, 256), bf16),
            pltpu.VMEM((20, 3, 96, 256), bf16),
            pltpu.VMEM((18, 3, 96, 256), bf16),
            pltpu.VMEM((18, 96, 256), f32),
            pltpu.VMEM((18, 3, 96, 256), bf16),
            pltpu.VMEM((96, 1824), bf16),
            pltpu.VMEM((96, 1664), f32),
            pltpu.VMEM((864, 128), bf16),
            pltpu.VMEM((2, 96, 128), bf16),
            pltpu.VMEM((2, 8, 96, 128), bf16),
            pltpu.SemaphoreType.DMA((7,)),
            pltpu.SemaphoreType.DMA((2, 10)),
            pltpu.SemaphoreType.DMA((2, 10)),
        ],
        compiler_params=pltpu.CompilerParams(
            collective_id=0, has_side_effects=True, vmem_limit_bytes=60 * 2**20
        ),
    )(features, teacher, w1, w2, wb, projector)


def shards(features, teacher, conv_in, conv_out, projector):
    return all_reduce(gradients(features, teacher, conv_in, conv_out, projector))


def solution(mesh):
    in_specs = (P(None, "row", "col"), P(None, "row", "col"), P(), P(), P())
    out_specs = (P(), P(), P())
    return jax.shard_map(shards, mesh=mesh, in_specs=in_specs, out_specs=out_specs, check_vma=False)
```

```python
import jax
import jax.numpy as jnp
from jax import lax
from jax.experimental import pallas as pl
from jax.experimental.pallas import tpu as pltpu
from jax.sharding import PartitionSpec as P

MESH = pl.DeviceIdType.MESH
ROWS = 3072


def place():
    row, col = lax.axis_index("row"), lax.axis_index("col")
    return dict(x=(row % 2) * 2 + col // 8, y=(col // 2) % 4, z=row // 2, core=col % 2)


def device(at, **moved):
    p = dict(at, **moved)
    return (p["z"] * 2 + p["x"] // 2, ((p["x"] % 2) * 4 + p["y"]) * 2 + p["core"])


def peers(at):
    yield device(at, core=1 - at["core"])
    for axis, n in (("x", 4), ("y", 4), ("z", 8)):
        for step in range(1, n):
            yield device(at, **{axis: (at[axis] + step) % n})


def al(x):
    return pl.multiple_of(x, 8)


def reduce_rows(at, v, r, base, count, bufs, sent, got):
    w, in0, in1, in2, out3, in3, sums3 = bufs
    half, colour, big, small, unit = (count // k for k in (2, 4, 16, 64, 256))
    orders = (("x", "y"), ("y", "x"))
    copies = []

    def copy(src, dst, peer):
        k = len(copies)
        c = pltpu.make_async_remote_copy(
            src_ref=src,
            dst_ref=dst,
            send_sem=sent.at[k],
            recv_sem=got.at[k],
            device_id=peer,
            device_id_type=MESH,
        )
        c.start()
        copies.append(c)
        return c

    core, z = at["core"], at["z"]
    other = device(at, core=1 - core)
    mine = al(base + core * half)
    c = copy(v.at[pl.ds(al(base + (1 - core) * half), half)], in0, other)
    yield
    c.wait_recv()
    w[...] = v[pl.ds(mine, half)] + in0[...]

    def scatter(starts, axes, size, into):
        out = []
        for k in range(2):
            for step in range(1, 4):
                q = (at[axes[k]] + step) % 4
                rows = pl.ds(al(starts[k] + q * size), size)
                out.append(copy(w.at[rows], into.at[k, step - 1], device(at, **{axes[k]: q})))
        return out

    waits = scatter((0, colour), ("x", "y"), big, in1)
    yield
    starts = []
    for k, axis in enumerate(("x", "y")):
        for c in waits[3 * k : 3 * k + 3]:
            c.wait_recv()
        starts.append(al(k * colour + at[axis] * big))
        rows = pl.ds(starts[k], big)
        w[rows] = w[rows] + in1[k, 0] + in1[k, 1] + in1[k, 2]
    waits = scatter(starts, ("y", "x"), small, in2)
    yield
    smalls = []
    for k, axis in enumerate(("y", "x")):
        for c in waits[3 * k : 3 * k + 3]:
            c.wait_recv()
        smalls.append(al(starts[k] + at[axis] * small))
        total = w[pl.ds(smalls[k], small)] + in2[k, 0] + in2[k, 1] + in2[k, 2]
        out3[k * 4 : k * 4 + 4] = total.reshape(4, unit, 128)
    waits = []
    for step in range(1, 8):
        q = (z + step) % 8
        waits.append(copy(out3.at[q], in3.at[step - 1], device(at, z=q)))
    yield
    total = out3[z]
    for k, c in enumerate(waits):
        c.wait_recv()
        total = total + in3[k]
    sums3[z] = total
    waits = []
    for step in range(1, 8):
        q = (z + step) % 8
        waits.append(copy(sums3.at[z], sums3.at[z], device(at, z=q)))
    yield
    for c in waits:
        c.wait_recv()
    waits = []
    for k, axis in enumerate(("y", "x")):
        rows = pl.ds(al(mine + smalls[k]), small)
        r[rows] = sums3[k * 4 : k * 4 + 4].reshape(small, 128)
        for step in range(1, 4):
            q = (at[axis] + step) % 4
            waits.append(copy(r.at[rows], r.at[rows], device(at, **{axis: q})))
    yield
    for c in waits:
        c.wait_recv()
    waits = []
    last = []
    for k, axis in enumerate(("x", "y")):
        rows = pl.ds(al(mine + starts[k]), big)
        for step in range(1, 4):
            q = (at[axis] + step) % 4
            waits.append(copy(r.at[rows], r.at[rows], device(at, **{axis: q})))
        last.append(copy(r.at[rows], r.at[rows], other))
    yield
    for k, axis in enumerate(("x", "y")):
        for step in range(1, 4):
            q = (at[axis] - step + 4) % 4
            rows = pl.ds(al(mine + k * colour + q * big), big)
            waits[3 * k + step - 1].wait_recv()
            last.append(copy(r.at[rows], r.at[rows], other))
    yield
    for c in last:
        c.wait_recv()
    for c in copies:
        c.wait_send()


def reduce_scratch(count):
    half, colour, big, small, unit = (count // k for k in (2, 4, 16, 64, 256))
    f32 = jnp.float32
    return [
        pltpu.VMEM((half, 128), f32),
        pltpu.VMEM((half, 128), f32),
        pltpu.VMEM((2, 3, big, 128), f32),
        pltpu.VMEM((2, 3, small, 128), f32),
        pltpu.VMEM((8, unit, 128), f32),
        pltpu.VMEM((7, unit, 128), f32),
        pltpu.VMEM((8, unit, 128), f32),
    ]


AROUND = ((-1, 0), (1, 0), (0, -1), (0, 1), (-1, -1), (-1, 1), (1, -1), (1, 1))
SCALE = 2.0**-20
CHUNK = 256


def dot(a, b):
    return jnp.dot(a, b, preferred_element_type=jnp.float32)


def dot_nt(a, b):
    return lax.dot_general(a, b, (((1,), (1,)), ((), ())), preferred_element_type=jnp.float32)


def pieces(value):
    out = []
    for _ in range(3):
        out.append(value.astype(jnp.bfloat16))
        value = value - out[-1].astype(jnp.float32)
    return out


def phi(value):
    return 0.5 * (1.0 + lax.erf(value * 0.7071067811865476))


def main_kernel(
    feat, teach, cin, cout, proj, gin, gout, gproj, v, r, sent_sum, got_sum,
    a0, a1, a2, a3, a4, a5, a6, b0, b1, b2, b3, b4, b5, b6,
    fv, cv, dv, p, tin, t2, xh, hh, gp, ds, w1, w2, wb, lhs, gacc, taps, tile, around, local, sent, got,
):
    bf16, f32 = jnp.bfloat16, jnp.float32
    rows, cols = lax.axis_size("row"), lax.axis_size("col")
    row, col = lax.axis_index("row"), lax.axis_index("col")
    up, down, left, right = row > 0, row < rows - 1, col > 0, col < cols - 1

    def neighbour(dr, dc):
        return ((row + dr + rows) % rows, (col + dc + cols) % cols)

    feat_copy = pltpu.make_async_copy(feat, fv, local.at[0])
    feat_copy.start()
    small = []
    for k, (src, dst) in enumerate(((cin, cv), (cout, dv), (proj, p))):
        small.append(pltpu.make_async_copy(src, dst, local.at[k + 7]))
        small[-1].start()
    t_copies = []
    for k in range(1536 // CHUNK):
        part = pl.ds(k * CHUNK, CHUNK)
        t_copies.append(pltpu.make_async_copy(teach.at[part], tin.at[part], local.at[k + 1]))
        t_copies[-1].start()
    barrier = pltpu.get_barrier_semaphore()
    place_here = place()
    greeted = [neighbour(dr, dc) for dr, dc in AROUND] + list(peers(place_here))
    for peer in greeted:
        pl.semaphore_signal(barrier, inc=1, device_id=peer, device_id_type=MESH)

    lane = lax.broadcasted_iota(jnp.int32, (96, 128), 1)
    hpos = (lane * 43) >> 8
    jpos = lane - hpos * 6

    def own_tile(read):
        acc = jnp.zeros((96, 128), f32)
        for h in range(16):
            x = read(h).astype(f32)
            at = (h + 2) * 6
            here = hpos == h + 2
            acc = jnp.where(here & (jpos < 2), pltpu.roll(x[:, 128:], at + 2, 1), acc)
            acc = jnp.where(here & (jpos > 3), pltpu.roll(x[:, :128], at + 4, 1), acc)
        return acc

    def exchange(part, top, bottom, to_top, to_bottom):
        copies = []

        def send(k, src, dst, dr, dc):
            c = pltpu.make_async_remote_copy(
                src_ref=src,
                dst_ref=dst,
                send_sem=sent.at[part, k],
                recv_sem=got.at[part, k],
                device_id=neighbour(dr, dc),
                device_id_type=MESH,
            )
            c.start()
            copies.append(c)

        send(8, top, to_bottom, -1, 0)
        send(9, bottom, to_top, 1, 0)
        for k, (dr, dc) in enumerate(AROUND):
            send(k, tile.at[part], around.at[part, AROUND.index((-dr, -dc))], dr, dc)
        return copies

    def rim(part):
        def get(dr, dc):
            if (dr, dc) == (0, 0):
                return tile[part].astype(f32)
            return around[part, AROUND.index((dr, dc))].astype(f32)

        def band(dr):
            mid = get(dr, 0)
            inner = jnp.where(jpos == 2, pltpu.roll(mid, 126, 1), pltpu.roll(mid, 2, 1))
            outer = jnp.where(jpos < 2, get(dr, -1), get(dr, 1))
            return jnp.where((jpos == 2) | (jpos == 3), inner, outer)

        full = jnp.where(
            hpos < 2,
            pltpu.roll(band(-1), 32, 1),
            jnp.where(hpos < 18, band(0), pltpu.roll(band(1), 96, 1)),
        )
        off = ((jpos < 2) & jnp.logical_not(left)) | ((jpos > 3) & jnp.logical_not(right))
        off = off | ((hpos < 2) & jnp.logical_not(up)) | ((hpos > 17) & jnp.logical_not(down))
        return jnp.where(off, 0.0, full)

    def shifted(buf, count, ahead, edge):
        def step(h, _):
            x = buf[h, 1].astype(f32)
            at = (h + ahead) * 6
            before = pltpu.roll(x, 1, 1)
            first = pltpu.roll(edge, 127 - at, 1)
            buf[h, 0, :, :128] = jnp.where(lane == 0, first, before[:, :128]).astype(bf16)
            buf[h, 0, :, 128:] = before[:, 128:].astype(bf16)
            after = pltpu.roll(x, 255, 1)
            last = pltpu.roll(edge, 123 - at, 1)
            buf[h, 2, :, :128] = after[:, :128].astype(bf16)
            buf[h, 2, :, 128:] = jnp.where(lane == 127, last, after[:, 128:]).astype(bf16)
            return 0

        lax.fori_loop(0, count, step, 0, unroll=2)

    def window(buf, h):
        return buf[pl.ds(h, 3)].reshape(864, 256)

    feat_copy.wait()

    def features(i, _):
        at = pl.multiple_of(i * 16, 16)
        xh[2:18, 1, pl.ds(at, 16), :] = jnp.swapaxes(fv[pl.ds(at, 16)], 0, 1)
        return 0

    lax.fori_loop(0, 6, features, 0)
    tile[0] = own_tile(lambda h: xh[h + 2, 1]).astype(bf16)
    pl.semaphore_wait(barrier, len(greeted))
    first = exchange(0, xh.at[2:4, 1], xh.at[16:18, 1], xh.at[0:2, 1], xh.at[18:20, 1])

    def relayout(i, _):
        at = pl.multiple_of(i * 16, 16)
        t2[:, pl.ds(at, 16), :] = jnp.swapaxes(tin[pl.ds(at, 16)], 0, 1)
        return 0

    for k, c in enumerate(t_copies):
        c.wait()
        lax.fori_loop(k * (CHUNK // 16), (k + 1) * (CHUNK // 16), relayout, 0)
    for c in small:
        c.wait()
    for dst, src in ((w1, cv), (w2, dv)):
        dst[...] = jnp.concatenate([src[t].astype(f32).T.astype(bf16) for t in range(9)], axis=1)
    wb[...] = jnp.concatenate([dv[8 - t] for t in range(9)], axis=1)
    lhs[...] = jnp.concatenate([-p[...]] + pieces(dot_nt(p[...], p[...])), axis=1)
    v[...] = jnp.zeros_like(v)
    gacc[...] = jnp.zeros_like(gacc)

    for c in first:
        c.wait_recv()

    @pl.when(jnp.logical_not(up))
    def _():
        xh[0:2, 1] = jnp.zeros((2, 96, 256), bf16)

    @pl.when(jnp.logical_not(down))
    def _():
        xh[18:20, 1] = jnp.zeros((2, 96, 256), bf16)

    edge = rim(0)
    shifted(xh, 20, 0, edge)

    for t in range(9):
        away = (t // 3 - 1) * 6 + t % 3 - 1
        taps[t * 96 : (t + 1) * 96] = pltpu.roll(edge, (128 - away) % 128, 1).astype(bf16)
    pre = dot(w1[...], taps[...])
    side = (pre * phi(pre)).astype(bf16).astype(f32)
    off = ((jpos < 2) & jnp.logical_not(left)) | ((jpos > 3) & jnp.logical_not(right))
    off = off | ((hpos < 2) & jnp.logical_not(up)) | ((hpos > 17) & jnp.logical_not(down))
    side = jnp.where(off, 0.0, side)

    def conv1(r, _):
        pre = dot(w1[...], window(xh, r))
        cdf = phi(pre)
        gp[r] = cdf + pre * (jnp.exp(-0.5 * pre * pre) * 0.3989422804014327)
        outside = ((r == 0) & jnp.logical_not(up)) | ((r == 17) & jnp.logical_not(down))
        hh[r, 1] = jnp.where(outside, 0.0, pre * cdf).astype(bf16)
        return 0

    lax.fori_loop(0, 18, conv1, 0, unroll=3)
    shifted(hh, 18, 1, side)

    def conv2(h, _):
        s = (xh[h + 2, 1].astype(f32) + dot(w2[...], window(hh, h))).astype(bf16)
        for k in range(3):
            t2[h, 1536 + k * 96 : 1632 + k * 96] = s
        ds[h + 1, 1] = (dot(lhs[...], t2[h]) * SCALE).astype(bf16)
        return 0

    lax.fori_loop(0, 16, conv2, 0, unroll=2)
    tile[1] = own_tile(lambda h: ds[h + 1, 1]).astype(bf16)
    second = exchange(1, ds.at[1, 1], ds.at[16, 1], ds.at[0, 1], ds.at[17, 1])

    def wide(read, h):
        return jnp.concatenate([read(h * 4 + k) for k in range(4)], axis=1)

    def grads(h, _):
        gacc[:, :96] += dot_nt(
            wide(lambda k: t2[k, :1632], h), wide(lambda k: t2[k, 1536:1632], h)
        )
        return 0

    def grads_out(h, _):
        v[:864, :96] += dot_nt(wide(lambda k: window(hh, k), h), wide(lambda k: ds[k + 1, 1], h))
        return 0

    lax.fori_loop(0, 4, grads, 0)
    mp = sum(dot(m, p[...]) for m in pieces(gacc[1536:1632, :96]))
    for k in range(12):
        part = slice(k * 128, (k + 1) * 128)
        v[864 + k * 96 : 960 + k * 96] = (mp[:, part] - gacc[part].T[:96]) * SCALE
    lax.fori_loop(0, 4, grads_out, 0)
    early = reduce_rows(
        place_here, v, r, 0, 2048, (a0, a1, a2, a3, a4, a5, a6), sent_sum.at[0], got_sum.at[0]
    )
    late = reduce_rows(
        place_here, v, r, 2048, 1024, (b0, b1, b2, b3, b4, b5, b6), sent_sum.at[1], got_sum.at[1]
    )
    next(early)

    for c in second:
        c.wait_recv()

    @pl.when(jnp.logical_not(up))
    def _():
        ds[0, 1] = jnp.zeros((96, 256), bf16)

    @pl.when(jnp.logical_not(down))
    def _():
        ds[17, 1] = jnp.zeros((96, 256), bf16)

    shifted(ds, 18, 1, rim(1))

    def back(h, _):
        def dpre(k):
            return (dot(wb[...], window(ds, k)) * gp[k + 1]).astype(bf16)

        v[2048:2912, :96] += dot_nt(wide(lambda k: window(xh, k + 1), h), wide(dpre, h))
        return 0

    next(early)
    lax.fori_loop(0, 2, back, 0)
    next(early)
    lax.fori_loop(2, 4, back, 0)
    next(late)
    for _ in range(5):
        next(early, None)
        next(late, None)
    next(early, None)
    for t in range(9):
        gout[t] = r[t * 96 : (t + 1) * 96, :96]
    for t in range(12):
        gproj[:, t * 128 : (t + 1) * 128] = r[864 + t * 96 : 960 + t * 96]
    for _ in late:
        pass
    for t in range(9):
        gin[t] = r[2048 + t * 96 : 2144 + t * 96, :96]
    for c in first + second:
        c.wait_send()


def gradients(features, teacher, conv_in, conv_out, projector):
    bf16, f32 = jnp.bfloat16, jnp.float32
    vmem = pl.BlockSpec(memory_space=pltpu.VMEM)
    hbm = pl.BlockSpec(memory_space=pl.ANY)
    return pl.pallas_call(
        main_kernel,
        out_shape=(
            jax.ShapeDtypeStruct((9, 96, 96), f32),
            jax.ShapeDtypeStruct((9, 96, 96), f32),
            jax.ShapeDtypeStruct((96, 1536), f32),
        ),
        in_specs=[hbm] * 5,
        out_specs=(vmem, vmem, vmem),
        scratch_shapes=[
            pltpu.VMEM((ROWS, 128), f32),
            pltpu.VMEM((ROWS, 128), f32),
            pltpu.SemaphoreType.DMA((2, 48)),
            pltpu.SemaphoreType.DMA((2, 48)),
            *reduce_scratch(2048),
            *reduce_scratch(1024),
            pltpu.VMEM((96, 16, 256), bf16),
            pltpu.VMEM((9, 96, 96), bf16),
            pltpu.VMEM((9, 96, 96), bf16),
            pltpu.VMEM((96, 1536), bf16),
            pltpu.VMEM((1536, 16, 256), bf16),
            pltpu.VMEM((16, 1824, 256), bf16),
            pltpu.VMEM((20, 3, 96, 256), bf16),
            pltpu.VMEM((18, 3, 96, 256), bf16),
            pltpu.VMEM((18, 96, 256), f32),
            pltpu.VMEM((18, 3, 96, 256), bf16),
            pltpu.VMEM((96, 864), bf16),
            pltpu.VMEM((96, 864), bf16),
            pltpu.VMEM((96, 864), bf16),
            pltpu.VMEM((96, 1824), bf16),
            pltpu.VMEM((1632, 128), f32),
            pltpu.VMEM((864, 128), bf16),
            pltpu.VMEM((2, 96, 128), bf16),
            pltpu.VMEM((2, 8, 96, 128), bf16),
            pltpu.SemaphoreType.DMA((10,)),
            pltpu.SemaphoreType.DMA((2, 10)),
            pltpu.SemaphoreType.DMA((2, 10)),
        ],
        compiler_params=pltpu.CompilerParams(
            collective_id=0, has_side_effects=True, vmem_limit_bytes=63 * 2**20
        ),
    )(features, teacher, conv_in, conv_out, projector)


def solution(mesh):
    in_specs = (P(None, "row", "col"), P(None, "row", "col"), P(), P(), P())
    out_specs = (P(), P(), P())
    return jax.shard_map(gradients, mesh=mesh, in_specs=in_specs, out_specs=out_specs, check_vma=False)
```

```python
import jax
import jax.numpy as jnp
from jax import lax
from jax.experimental import pallas as pl
from jax.experimental.pallas import tpu as pltpu
from jax.sharding import PartitionSpec as P

MESH = pl.DeviceIdType.MESH
ROWS = 3072


def place():
    row, col = lax.axis_index("row"), lax.axis_index("col")
    return dict(x=(row % 2) * 2 + col // 8, y=(col // 2) % 4, z=row // 2, core=col % 2)


def device(at, **moved):
    p = dict(at, **moved)
    return (p["z"] * 2 + p["x"] // 2, ((p["x"] % 2) * 4 + p["y"]) * 2 + p["core"])


def peers(at):
    yield device(at, core=1 - at["core"])
    for axis, n in (("x", 4), ("y", 4), ("z", 8)):
        for step in range(1, n):
            yield device(at, **{axis: (at[axis] + step) % n})


def al(x):
    return pl.multiple_of(x, 8)


def reduce_rows(at, v, r, base, count, bufs, sent, got):
    w, in0, in1, in2, out3, in3, sums3 = bufs
    half, colour, big, small, unit = (count // k for k in (2, 4, 16, 64, 256))
    orders = (("x", "y"), ("y", "x"))
    copies = []

    def copy(src, dst, peer):
        k = len(copies)
        c = pltpu.make_async_remote_copy(
            src_ref=src,
            dst_ref=dst,
            send_sem=sent.at[k],
            recv_sem=got.at[k],
            device_id=peer,
            device_id_type=MESH,
        )
        c.start()
        copies.append(c)
        return c

    core, z = at["core"], at["z"]
    other = device(at, core=1 - core)
    mine = al(base + core * half)
    c = copy(v.at[pl.ds(al(base + (1 - core) * half), half)], in0, other)
    yield
    c.wait_recv()
    w[...] = v[pl.ds(mine, half)] + in0[...]

    def scatter(starts, axes, size, into):
        out = []
        for k in range(2):
            for step in range(1, 4):
                q = (at[axes[k]] + step) % 4
                rows = pl.ds(al(starts[k] + q * size), size)
                out.append(copy(w.at[rows], into.at[k, step - 1], device(at, **{axes[k]: q})))
        return out

    waits = scatter((0, colour), ("x", "y"), big, in1)
    yield
    starts = []
    for k, axis in enumerate(("x", "y")):
        for c in waits[3 * k : 3 * k + 3]:
            c.wait_recv()
        starts.append(al(k * colour + at[axis] * big))
        rows = pl.ds(starts[k], big)
        w[rows] = w[rows] + in1[k, 0] + in1[k, 1] + in1[k, 2]
    waits = scatter(starts, ("y", "x"), small, in2)
    yield
    smalls = []
    for k, axis in enumerate(("y", "x")):
        for c in waits[3 * k : 3 * k + 3]:
            c.wait_recv()
        smalls.append(al(starts[k] + at[axis] * small))
        total = w[pl.ds(smalls[k], small)] + in2[k, 0] + in2[k, 1] + in2[k, 2]
        out3[k * 4 : k * 4 + 4] = total.reshape(4, unit, 128)
    waits = []
    for step in range(1, 8):
        q = (z + step) % 8
        waits.append(copy(out3.at[q], in3.at[step - 1], device(at, z=q)))
    yield
    total = out3[z]
    for k, c in enumerate(waits):
        c.wait_recv()
        total = total + in3[k]
    sums3[z] = total
    waits = []
    for step in range(1, 8):
        q = (z + step) % 8
        waits.append(copy(sums3.at[z], sums3.at[z], device(at, z=q)))
    yield
    for c in waits:
        c.wait_recv()
    waits = []
    for k, axis in enumerate(("y", "x")):
        rows = pl.ds(al(mine + smalls[k]), small)
        r[rows] = sums3[k * 4 : k * 4 + 4].reshape(small, 128)
        for step in range(1, 4):
            q = (at[axis] + step) % 4
            waits.append(copy(r.at[rows], r.at[rows], device(at, **{axis: q})))
    yield
    for c in waits:
        c.wait_recv()
    waits = []
    last = []
    for k, axis in enumerate(("x", "y")):
        rows = pl.ds(al(mine + starts[k]), big)
        for step in range(1, 4):
            q = (at[axis] + step) % 4
            waits.append(copy(r.at[rows], r.at[rows], device(at, **{axis: q})))
        last.append(copy(r.at[rows], r.at[rows], other))
    yield
    for k, axis in enumerate(("x", "y")):
        for step in range(1, 4):
            q = (at[axis] - step + 4) % 4
            rows = pl.ds(al(mine + k * colour + q * big), big)
            waits[3 * k + step - 1].wait_recv()
            last.append(copy(r.at[rows], r.at[rows], other))
    yield
    for c in last:
        c.wait_recv()
    for c in copies:
        c.wait_send()


def reduce_scratch(count):
    half, colour, big, small, unit = (count // k for k in (2, 4, 16, 64, 256))
    f32 = jnp.float32
    return [
        pltpu.VMEM((half, 128), f32),
        pltpu.VMEM((half, 128), f32),
        pltpu.VMEM((2, 3, big, 128), f32),
        pltpu.VMEM((2, 3, small, 128), f32),
        pltpu.VMEM((8, unit, 128), f32),
        pltpu.VMEM((7, unit, 128), f32),
        pltpu.VMEM((8, unit, 128), f32),
    ]


AROUND = ((-1, 0), (1, 0), (0, -1), (0, 1), (-1, -1), (-1, 1), (1, -1), (1, 1))
SCALE = 2.0**-20
CHUNK = 256


def dot(a, b):
    return jnp.dot(a, b, preferred_element_type=jnp.float32)


def dot_nt(a, b):
    return lax.dot_general(a, b, (((1,), (1,)), ((), ())), preferred_element_type=jnp.float32)


def pieces(value):
    out = []
    for _ in range(3):
        out.append(value.astype(jnp.bfloat16))
        value = value - out[-1].astype(jnp.float32)
    return out


def phi(value):
    return 0.5 * (1.0 + lax.erf(value * 0.7071067811865476))


def main_kernel(
    feat, teach, cin, cout, proj, r, v, sent_sum, got_sum,
    a0, a1, a2, a3, a4, a5, a6, b0, b1, b2, b3, b4, b5, b6, c0, c1, c2, c3, c4, c5, c6,
    fv, cv, dv, p, tin, t2, xh, hh, gp, ds, w1, w2, wb, lhs, gacc, taps, tile, around, local, sent, got,
):
    bf16, f32 = jnp.bfloat16, jnp.float32
    rows, cols = lax.axis_size("row"), lax.axis_size("col")
    row, col = lax.axis_index("row"), lax.axis_index("col")
    up, down, left, right = row > 0, row < rows - 1, col > 0, col < cols - 1

    def neighbour(dr, dc):
        return ((row + dr + rows) % rows, (col + dc + cols) % cols)

    feat_copy = pltpu.make_async_copy(feat, fv, local.at[0])
    feat_copy.start()
    small = []
    for k, (src, dst) in enumerate(((cin, cv), (cout, dv), (proj, p))):
        small.append(pltpu.make_async_copy(src, dst, local.at[k + 7]))
        small[-1].start()
    t_copies = []
    for k in range(1536 // CHUNK):
        part = pl.ds(k * CHUNK, CHUNK)
        t_copies.append(pltpu.make_async_copy(teach.at[part], tin.at[part], local.at[k + 1]))
        t_copies[-1].start()
    barrier = pltpu.get_barrier_semaphore()
    place_here = place()
    greeted = [neighbour(dr, dc) for dr, dc in AROUND] + list(peers(place_here))
    for peer in greeted:
        pl.semaphore_signal(barrier, inc=1, device_id=peer, device_id_type=MESH)

    lane = lax.broadcasted_iota(jnp.int32, (96, 128), 1)
    hpos = (((lane + 2) * 43) >> 8) - 1
    jpos = lane - 4 - hpos * 6
    off = ((jpos < 2) & jnp.logical_not(left)) | ((jpos > 3) & jnp.logical_not(right))
    off = off | ((hpos < 2) & jnp.logical_not(up)) | ((hpos > 17) & jnp.logical_not(down))

    def own_tile(read):
        acc = jnp.zeros((96, 128), f32)
        for h in range(16):
            x = read(h).astype(f32)
            at = (h + 2) * 6 + 4
            here = hpos == h + 2
            acc = jnp.where(here & (jpos < 2), pltpu.roll(x[:, 128:], at + 2, 1), acc)
            acc = jnp.where(here & (jpos > 3), pltpu.roll(x[:, :128], at + 4, 1), acc)
        return jnp.concatenate([acc, jnp.zeros((32, 128), f32)]).T.astype(bf16)

    def exchange(part, top, bottom, to_top, to_bottom):
        def send(k, src, dst, dr, dc):
            c = pltpu.make_async_remote_copy(
                src_ref=src,
                dst_ref=dst,
                send_sem=sent.at[part, k],
                recv_sem=got.at[part, k],
                device_id=neighbour(dr, dc),
                device_id_type=MESH,
            )
            c.start()
            return c

        def send_tile(k):
            dr, dc = AROUND[k]
            lines = (slice(16, 112), slice(96, 112), slice(16, 32))[dr]
            return send(
                k,
                tile.at[part, lines],
                around.at[part, AROUND.index((-dr, -dc)), lines],
                dr,
                dc,
            )

        sides = [send_tile(2), send_tile(3)]
        rest = [send(8, top, to_bottom, -1, 0), send(9, bottom, to_top, 1, 0)]
        rest += [send_tile(k) for k in (0, 1, 4, 5, 6, 7)]
        return sides, rest

    def rim(part, whole):
        def column(dc):
            def piece(dr, lines):
                if (dr, dc) == (0, 0):
                    return tile[part, lines]
                return around[part, AROUND.index((dr, dc)), lines]

            above = below = jnp.zeros((16, 128), bf16)
            if whole:
                above, below = piece(-1, slice(96, 112)), piece(1, slice(16, 32))
            lines = jnp.concatenate([above, piece(0, slice(16, 112)), below])
            return lines.astype(f32).T[:96]

        mid = column(0)
        inner = jnp.where(jpos == 2, pltpu.roll(mid, 126, 1), pltpu.roll(mid, 2, 1))
        outer = jnp.where(jpos < 2, column(-1), column(1))
        full = jnp.where((jpos == 2) | (jpos == 3), inner, outer)
        return jnp.where(off, 0.0, full)

    def shift_row(buf, h, ahead, edge):
        x = buf[h, 1].astype(f32)
        at = (h + ahead) * 6
        before = pltpu.roll(x, 1, 1)
        first = pltpu.roll(edge, 123 - at, 1)
        buf[h, 0, :, :128] = jnp.where(lane == 0, first, before[:, :128]).astype(bf16)
        buf[h, 0, :, 128:] = before[:, 128:].astype(bf16)
        after = pltpu.roll(x, 255, 1)
        last = pltpu.roll(edge, 119 - at, 1)
        buf[h, 2, :, :128] = after[:, :128].astype(bf16)
        buf[h, 2, :, 128:] = jnp.where(lane == 127, last, after[:, 128:]).astype(bf16)

    def shifted(buf, start, stop, ahead, edge):
        def step(h, _):
            shift_row(buf, h, ahead, edge)
            return 0

        lax.fori_loop(start, stop, step, 0, unroll=2)

    def window(buf, h):
        return buf[pl.ds(h, 3)].reshape(864, 256)

    feat_copy.wait()

    def features(i, _):
        at = pl.multiple_of(i * 16, 16)
        xh[2:18, 1, pl.ds(at, 16), :] = jnp.swapaxes(fv[pl.ds(at, 16)], 0, 1)
        return 0

    lax.fori_loop(0, 6, features, 0)
    tile[0] = own_tile(lambda h: xh[h + 2, 1])
    pl.semaphore_wait(barrier, len(greeted))
    first_sides, first = exchange(0, xh.at[2:4, 1], xh.at[16:18, 1], xh.at[0:2, 1], xh.at[18:20, 1])

    def relayout(i, _):
        at = pl.multiple_of(i * 16, 16)
        t2[:, pl.ds(at, 16), :] = jnp.swapaxes(tin[pl.ds(at, 16)], 0, 1)
        return 0

    for k, c in enumerate(t_copies):
        c.wait()
        lax.fori_loop(k * (CHUNK // 16), (k + 1) * (CHUNK // 16), relayout, 0)
    for c in small:
        c.wait()
    for dst, src in ((w1, cv), (w2, dv)):
        dst[...] = jnp.concatenate([src[t].astype(f32).T.astype(bf16) for t in range(9)], axis=1)
    wb[...] = jnp.concatenate([dv[8 - t] for t in range(9)], axis=1)
    lhs[...] = jnp.concatenate([-p[...]] + pieces(dot_nt(p[...], p[...])), axis=1)
    v[...] = jnp.zeros_like(v)
    gacc[...] = jnp.zeros_like(gacc)

    def conv1(r, _):
        pre = dot(w1[...], window(xh, r))
        cdf = phi(pre)
        gp[r] = cdf + pre * (jnp.exp(-0.5 * pre * pre) * 0.3989422804014327)
        outside = ((r == 0) & jnp.logical_not(up)) | ((r == 17) & jnp.logical_not(down))
        hh[r, 1] = jnp.where(outside, 0.0, pre * cdf).astype(bf16)
        return 0

    for c in first_sides:
        c.wait_recv()
    shifted(xh, 2, 18, 0, rim(0, False))
    lax.fori_loop(2, 16, conv1, 0, unroll=2)

    for c in first:
        c.wait_recv()

    @pl.when(jnp.logical_not(up))
    def _():
        xh[0:2, 1] = jnp.zeros((2, 96, 256), bf16)

    @pl.when(jnp.logical_not(down))
    def _():
        xh[18:20, 1] = jnp.zeros((2, 96, 256), bf16)

    edge = rim(0, True)
    for h in (0, 1, 18, 19):
        shift_row(xh, h, 0, edge)
    for line in (0, 1, 16, 17):
        conv1(line, 0)

    for t in range(9):
        away = (t // 3 - 1) * 6 + t % 3 - 1
        taps[t * 96 : (t + 1) * 96] = pltpu.roll(edge, (128 - away) % 128, 1).astype(bf16)
    pre = dot(w1[...], taps[...])
    side = jnp.where(off, 0.0, (pre * phi(pre)).astype(bf16).astype(f32))
    shifted(hh, 0, 18, 1, side)

    def conv2(h, _):
        s = (xh[h + 2, 1].astype(f32) + dot(w2[...], window(hh, h))).astype(bf16)
        for k in range(3):
            t2[h, 1536 + k * 96 : 1632 + k * 96] = s
        ds[h + 1, 1] = (dot(lhs[...], t2[h]) * SCALE).astype(bf16)
        return 0

    lax.fori_loop(0, 16, conv2, 0, unroll=2)
    tile[1] = own_tile(lambda h: ds[h + 1, 1])
    second_sides, second = exchange(1, ds.at[1, 1], ds.at[16, 1], ds.at[0, 1], ds.at[17, 1])

    def wide(read, h):
        return jnp.concatenate([read(h * 4 + k) for k in range(4)], axis=1)

    def grads(h, _):
        gacc[:, :96] += dot_nt(
            wide(lambda k: t2[k, :1632], h), wide(lambda k: t2[k, 1536:1632], h)
        )
        return 0

    def grads_out(h, _):
        v[1152:2016, :96] += dot_nt(wide(lambda k: window(hh, k), h), wide(lambda k: ds[k + 1, 1], h))
        return 0

    lax.fori_loop(0, 4, grads, 0)
    mp = sum(dot(m, p[...]) for m in pieces(gacc[1536:1632, :96]))
    for k in range(12):
        part = slice(k * 128, (k + 1) * 128)
        v[k * 96 : 96 + k * 96] = (mp[:, part] - gacc[part].T[:96]) * SCALE
    sums = {
        name: reduce_rows(
            place_here, v, r, k * 1024, 1024, bufs, sent_sum.at[k], got_sum.at[k]
        )
        for k, (name, bufs) in enumerate(
            (
                ("E", (a0, a1, a2, a3, a4, a5, a6)),
                ("M", (b0, b1, b2, b3, b4, b5, b6)),
                ("L", (c0, c1, c2, c3, c4, c5, c6)),
            )
        )
    }
    next(sums["E"])

    for c in second_sides + second:
        c.wait_recv()

    @pl.when(jnp.logical_not(up))
    def _():
        ds[0, 1] = jnp.zeros((96, 256), bf16)

    @pl.when(jnp.logical_not(down))
    def _():
        ds[17, 1] = jnp.zeros((96, 256), bf16)

    shifted(ds, 0, 18, 1, rim(1, True))

    def back(h, _):
        def dpre(k):
            return (dot(wb[...], window(ds, k)) * gp[k + 1]).astype(bf16)

        v[2048:2912, :96] += dot_nt(wide(lambda k: window(xh, k + 1), h), wide(dpre, h))
        return 0

    next(sums["E"])
    lax.fori_loop(0, 4, back, 0)
    next(sums["L"])
    next(sums["E"])
    lax.fori_loop(0, 2, grads_out, 0)
    next(sums["L"])
    lax.fori_loop(2, 4, grads_out, 0)
    for name in "MEMLEMLMELEMLEMLEM":
        next(sums[name], None)
    for _ in sums["L"]:
        pass
    for name in "EM":
        for _ in sums[name]:
            pass
    for c in first_sides + first + second_sides + second:
        c.wait_send()


def finish(r, gin, gout, gproj):
    for t in range(12):
        gproj[:, t * 128 : (t + 1) * 128] = r[t * 96 : 96 + t * 96]
    for t in range(9):
        gout[t] = r[1152 + t * 96 : 1248 + t * 96, :96]
        gin[t] = r[2048 + t * 96 : 2144 + t * 96, :96]


def gradients(features, teacher, conv_in, conv_out, projector):
    bf16, f32 = jnp.bfloat16, jnp.float32
    vmem = pl.BlockSpec(memory_space=pltpu.VMEM)
    hbm = pl.BlockSpec(memory_space=pltpu.HBM)
    sums = pl.pallas_call(
        main_kernel,
        out_shape=jax.ShapeDtypeStruct((ROWS, 128), f32),
        in_specs=[hbm] * 5,
        out_specs=vmem,
        scratch_shapes=[
            pltpu.VMEM((ROWS, 128), f32),
            pltpu.SemaphoreType.DMA((3, 48)),
            pltpu.SemaphoreType.DMA((3, 48)),
            *reduce_scratch(1024),
            *reduce_scratch(1024),
            *reduce_scratch(1024),
            pltpu.VMEM((96, 16, 256), bf16),
            pltpu.VMEM((9, 96, 96), bf16),
            pltpu.VMEM((9, 96, 96), bf16),
            pltpu.VMEM((96, 1536), bf16),
            pltpu.VMEM((1536, 16, 256), bf16),
            pltpu.VMEM((16, 1824, 256), bf16),
            pltpu.VMEM((20, 3, 96, 256), bf16),
            pltpu.VMEM((18, 3, 96, 256), bf16),
            pltpu.VMEM((18, 96, 256), f32),
            pltpu.VMEM((18, 3, 96, 256), bf16),
            pltpu.VMEM((96, 864), bf16),
            pltpu.VMEM((96, 864), bf16),
            pltpu.VMEM((96, 864), bf16),
            pltpu.VMEM((96, 1824), bf16),
            pltpu.VMEM((1632, 128), f32),
            pltpu.VMEM((864, 128), bf16),
            pltpu.VMEM((2, 128, 128), bf16),
            pltpu.VMEM((2, 8, 128, 128), bf16),
            pltpu.SemaphoreType.DMA((10,)),
            pltpu.SemaphoreType.DMA((2, 10)),
            pltpu.SemaphoreType.DMA((2, 10)),
        ],
        compiler_params=pltpu.CompilerParams(
            collective_id=0, has_side_effects=True, vmem_limit_bytes=62 * 2**20
        ),
    )(features, teacher, conv_in, conv_out, projector)
    return pl.pallas_call(
        finish,
        out_shape=(
            jax.ShapeDtypeStruct((9, 96, 96), f32),
            jax.ShapeDtypeStruct((9, 96, 96), f32),
            jax.ShapeDtypeStruct((96, 1536), f32),
        ),
        in_specs=[vmem],
        out_specs=(vmem, vmem, vmem),
    )(sums)


def solution(mesh):
    in_specs = (P(None, "row", "col"), P(None, "row", "col"), P(), P(), P())
    out_specs = (P(), P(), P())
    return jax.shard_map(gradients, mesh=mesh, in_specs=in_specs, out_specs=out_specs, check_vma=False)
```

```python
import jax
import jax.numpy as jnp
from jax import lax
from jax.experimental import pallas as pl
from jax.experimental.pallas import tpu as pltpu
from jax.sharding import PartitionSpec as P

MESH = pl.DeviceIdType.MESH
ROWS = 3072


def place():
    row, col = lax.axis_index("row"), lax.axis_index("col")
    return dict(x=(row % 2) * 2 + col // 8, y=(col // 2) % 4, z=row // 2, core=col % 2)


def device(at, **moved):
    p = dict(at, **moved)
    return (p["z"] * 2 + p["x"] // 2, ((p["x"] % 2) * 4 + p["y"]) * 2 + p["core"])


def peers(at):
    yield device(at, core=1 - at["core"])
    for axis, n in (("x", 4), ("y", 4), ("z", 8)):
        for step in range(1, n):
            yield device(at, **{axis: (at[axis] + step) % n})
    for axis in "xy":
        for step in range(1, 4):
            yield device(at, **{axis: (at[axis] + step) % 4, "core": 1 - at["core"]})


def al(x):
    return pl.multiple_of(x, 8)


def reduce_rows(at, v, r, base, count, bufs, sent, got, short):
    w, in0, in1, in2, out3, in3, sums3 = bufs
    half, colour, big, small, unit = (count // k for k in (2, 4, 16, 64, 256))
    orders = (("x", "y"), ("y", "x"))
    copies = []

    def copy(src, dst, peer):
        k = len(copies)
        c = pltpu.make_async_remote_copy(
            src_ref=src,
            dst_ref=dst,
            send_sem=sent.at[k],
            recv_sem=got.at[k],
            device_id=peer,
            device_id_type=MESH,
        )
        c.start()
        copies.append(c)
        return c

    core, z = at["core"], at["z"]
    other = device(at, core=1 - core)
    mine = al(base + core * half)
    c = copy(v.at[pl.ds(al(base + (1 - core) * half), half)], in0, other)
    yield
    c.wait_recv()
    w[...] = v[pl.ds(mine, half)] + in0[...]

    def scatter(starts, axes, size, into):
        out = []
        for k in range(2):
            for step in range(1, 4):
                q = (at[axes[k]] + step) % 4
                rows = pl.ds(al(starts[k] + q * size), size)
                out.append(copy(w.at[rows], into.at[k, step - 1], device(at, **{axes[k]: q})))
        return out

    waits = scatter((0, colour), ("x", "y"), big, in1)
    yield
    starts = []
    for k, axis in enumerate(("x", "y")):
        for c in waits[3 * k : 3 * k + 3]:
            c.wait_recv()
        starts.append(al(k * colour + at[axis] * big))
        rows = pl.ds(starts[k], big)
        w[rows] = w[rows] + in1[k, 0] + in1[k, 1] + in1[k, 2]
    waits = scatter(starts, ("y", "x"), small, in2)
    yield
    smalls = []
    for k, axis in enumerate(("y", "x")):
        for c in waits[3 * k : 3 * k + 3]:
            c.wait_recv()
        smalls.append(al(starts[k] + at[axis] * small))
        total = w[pl.ds(smalls[k], small)] + in2[k, 0] + in2[k, 1] + in2[k, 2]
        out3[k * 4 : k * 4 + 4] = total.reshape(4, unit, 128)
    if short:
        in3[z] = out3[...]
        waits = []
        for step in range(1, 8):
            waits.append(copy(out3, in3.at[z], device(at, z=(z + step) % 8)))
        yield
        for c in waits:
            c.wait_recv()
        total = in3[0]
        for k in range(1, 8):
            total = total + in3[k]
        sums3[...] = total
    else:
        waits = []
        for step in range(1, 8):
            q = (z + step) % 8
            waits.append(copy(out3.at[q], in3.at[step - 1], device(at, z=q)))
        yield
        total = out3[z]
        for k, c in enumerate(waits):
            c.wait_recv()
            total = total + in3[k]
        sums3[z] = total
        waits = []
        for step in range(1, 8):
            q = (z + step) % 8
            waits.append(copy(sums3.at[z], sums3.at[z], device(at, z=q)))
        yield
        for c in waits:
            c.wait_recv()
    waits = []
    for k, axis in enumerate(("y", "x")):
        rows = pl.ds(al(mine + smalls[k]), small)
        r[rows] = sums3[k * 4 : k * 4 + 4].reshape(small, 128)
        for step in range(1, 4):
            q = (at[axis] + step) % 4
            waits.append(copy(r.at[rows], r.at[rows], device(at, **{axis: q})))
    yield
    for c in waits:
        c.wait_recv()
    waits = []
    last = []
    for k, axis in enumerate(("x", "y")):
        rows = pl.ds(al(mine + starts[k]), big)
        for step in range(1, 4):
            q = (at[axis] + step) % 4
            waits.append(copy(r.at[rows], r.at[rows], device(at, **{axis: q})))
        last.append(copy(r.at[rows], r.at[rows], other))
        if short:
            for step in range(1, 4):
                peer = device(at, **{axis: (at[axis] + step) % 4, "core": 1 - core})
                last.append(copy(r.at[rows], r.at[rows], peer))
    yield
    if short:
        last += waits
    for k, axis in enumerate(() if short else ("x", "y")):
        for step in range(1, 4):
            q = (at[axis] - step + 4) % 4
            rows = pl.ds(al(mine + k * colour + q * big), big)
            waits[3 * k + step - 1].wait_recv()
            last.append(copy(r.at[rows], r.at[rows], other))
    if not short:
        yield
    for c in last:
        c.wait_recv()
    for c in copies:
        c.wait_send()


def reduce_scratch(count, short):
    half, colour, big, small, unit = (count // k for k in (2, 4, 16, 64, 256))
    f32 = jnp.float32
    return [
        pltpu.VMEM((half, 128), f32),
        pltpu.VMEM((half, 128), f32),
        pltpu.VMEM((2, 3, big, 128), f32),
        pltpu.VMEM((2, 3, small, 128), f32),
        pltpu.VMEM((8, unit, 128), f32),
        pltpu.VMEM((8, 8, unit, 128) if short else (7, unit, 128), f32),
        pltpu.VMEM((8, unit, 128), f32),
    ]


AROUND = ((-1, 0), (1, 0), (0, -1), (0, 1), (-1, -1), (-1, 1), (1, -1), (1, 1))
SCALE = 2.0**-20
CHUNK = 256


def dot(a, b):
    return jnp.dot(a, b, preferred_element_type=jnp.float32)


def dot_nt(a, b):
    return lax.dot_general(a, b, (((1,), (1,)), ((), ())), preferred_element_type=jnp.float32)


def pieces(value):
    out = []
    for _ in range(3):
        out.append(value.astype(jnp.bfloat16))
        value = value - out[-1].astype(jnp.float32)
    return out


def phi(value):
    return 0.5 * (1.0 + lax.erf(value * 0.7071067811865476))


def main_kernel(
    feat, teach, cin, cout, proj, r, v, sent_sum, got_sum,
    a0, a1, a2, a3, a4, a5, a6, b0, b1, b2, b3, b4, b5, b6, c0, c1, c2, c3, c4, c5, c6,
    fv, cv, dv, p, tin, t2, xh, hh, gp, ds, w1, w2, wb, lhs, gacc, taps, tile, around, local, sent, got,
):
    bf16, f32 = jnp.bfloat16, jnp.float32
    rows, cols = lax.axis_size("row"), lax.axis_size("col")
    row, col = lax.axis_index("row"), lax.axis_index("col")
    up, down, left, right = row > 0, row < rows - 1, col > 0, col < cols - 1

    def neighbour(dr, dc):
        return ((row + dr + rows) % rows, (col + dc + cols) % cols)

    feat_copy = pltpu.make_async_copy(feat, fv, local.at[0])
    feat_copy.start()
    small = []
    for k, (src, dst) in enumerate(((cin, cv), (cout, dv), (proj, p))):
        small.append(pltpu.make_async_copy(src, dst, local.at[k + 7]))
        small[-1].start()
    t_copies = []
    for k in range(1536 // CHUNK):
        part = pl.ds(k * CHUNK, CHUNK)
        t_copies.append(pltpu.make_async_copy(teach.at[part], tin.at[part], local.at[k + 1]))
        t_copies[-1].start()
    barrier = pltpu.get_barrier_semaphore()
    place_here = place()
    greeted = [neighbour(dr, dc) for dr, dc in AROUND] + list(peers(place_here))
    for peer in greeted:
        pl.semaphore_signal(barrier, inc=1, device_id=peer, device_id_type=MESH)

    lane = lax.broadcasted_iota(jnp.int32, (96, 128), 1)
    hpos = (((lane + 2) * 43) >> 8) - 1
    jpos = lane - 4 - hpos * 6
    off = ((jpos < 2) & jnp.logical_not(left)) | ((jpos > 3) & jnp.logical_not(right))
    off = off | ((hpos < 2) & jnp.logical_not(up)) | ((hpos > 17) & jnp.logical_not(down))

    def own_tile(read):
        acc = jnp.zeros((96, 128), f32)
        for h in range(16):
            x = read(h).astype(f32)
            at = (h + 2) * 6 + 4
            here = hpos == h + 2
            acc = jnp.where(here & (jpos < 2), pltpu.roll(x[:, 128:], at + 2, 1), acc)
            acc = jnp.where(here & (jpos > 3), pltpu.roll(x[:, :128], at + 4, 1), acc)
        return jnp.concatenate([acc, jnp.zeros((32, 128), f32)]).T.astype(bf16)

    def exchange(part, top, bottom, to_top, to_bottom):
        def send(k, src, dst, dr, dc):
            c = pltpu.make_async_remote_copy(
                src_ref=src,
                dst_ref=dst,
                send_sem=sent.at[part, k],
                recv_sem=got.at[part, k],
                device_id=neighbour(dr, dc),
                device_id_type=MESH,
            )
            c.start()
            return c

        def send_tile(k):
            dr, dc = AROUND[k]
            lines = (slice(16, 112), slice(96, 112), slice(16, 32))[dr]
            return send(
                k,
                tile.at[part, lines],
                around.at[part, AROUND.index((-dr, -dc)), lines],
                dr,
                dc,
            )

        sides = [send_tile(2), send_tile(3)]
        rest = [send(8, top, to_bottom, -1, 0), send(9, bottom, to_top, 1, 0)]
        rest += [send_tile(k) for k in (0, 1, 4, 5, 6, 7)]
        return sides, rest

    def rim(part, whole):
        def column(dc):
            def piece(dr, lines):
                if (dr, dc) == (0, 0):
                    return tile[part, lines]
                return around[part, AROUND.index((dr, dc)), lines]

            above = below = jnp.zeros((16, 128), bf16)
            if whole:
                above, below = piece(-1, slice(96, 112)), piece(1, slice(16, 32))
            lines = jnp.concatenate([above, piece(0, slice(16, 112)), below])
            return lines.astype(f32).T[:96]

        mid = column(0)
        inner = jnp.where(jpos == 2, pltpu.roll(mid, 126, 1), pltpu.roll(mid, 2, 1))
        outer = jnp.where(jpos < 2, column(-1), column(1))
        full = jnp.where((jpos == 2) | (jpos == 3), inner, outer)
        return jnp.where(off, 0.0, full)

    def shift_row(buf, h, ahead, edge):
        x = buf[h, 1].astype(f32)
        at = (h + ahead) * 6
        before = pltpu.roll(x, 1, 1)
        first = pltpu.roll(edge, 123 - at, 1)
        buf[h, 0, :, :128] = jnp.where(lane == 0, first, before[:, :128]).astype(bf16)
        buf[h, 0, :, 128:] = before[:, 128:].astype(bf16)
        after = pltpu.roll(x, 255, 1)
        last = pltpu.roll(edge, 119 - at, 1)
        buf[h, 2, :, :128] = after[:, :128].astype(bf16)
        buf[h, 2, :, 128:] = jnp.where(lane == 127, last, after[:, 128:]).astype(bf16)

    def shifted(buf, start, stop, ahead, edge):
        def step(h, _):
            shift_row(buf, h, ahead, edge)
            return 0

        lax.fori_loop(start, stop, step, 0, unroll=2)

    def window(buf, h):
        return buf[pl.ds(h, 3)].reshape(864, 256)

    feat_copy.wait()

    def features(i, _):
        at = pl.multiple_of(i * 16, 16)
        xh[2:18, 1, pl.ds(at, 16), :] = jnp.swapaxes(fv[pl.ds(at, 16)], 0, 1)
        return 0

    lax.fori_loop(0, 6, features, 0)
    tile[0] = own_tile(lambda h: xh[h + 2, 1])
    pl.semaphore_wait(barrier, len(greeted))
    first_sides, first = exchange(0, xh.at[2:4, 1], xh.at[16:18, 1], xh.at[0:2, 1], xh.at[18:20, 1])

    def relayout(i, _):
        at = pl.multiple_of(i * 16, 16)
        t2[:, pl.ds(at, 16), :] = jnp.swapaxes(tin[pl.ds(at, 16)], 0, 1)
        return 0

    for k, c in enumerate(t_copies):
        c.wait()
        lax.fori_loop(k * (CHUNK // 16), (k + 1) * (CHUNK // 16), relayout, 0)
    for c in small:
        c.wait()
    for dst, src in ((w1, cv), (w2, dv)):
        dst[...] = jnp.concatenate([src[t].astype(f32).T.astype(bf16) for t in range(9)], axis=1)
    wb[...] = jnp.concatenate([dv[8 - t] for t in range(9)], axis=1)
    lhs[...] = jnp.concatenate([-p[...]] + pieces(dot_nt(p[...], p[...])), axis=1)
    v[...] = jnp.zeros_like(v)
    gacc[...] = jnp.zeros_like(gacc)

    def conv1(r, _):
        pre = dot(w1[...], window(xh, r))
        cdf = phi(pre)
        gp[r] = cdf + pre * (jnp.exp(-0.5 * pre * pre) * 0.3989422804014327)
        outside = ((r == 0) & jnp.logical_not(up)) | ((r == 17) & jnp.logical_not(down))
        hh[r, 1] = jnp.where(outside, 0.0, pre * cdf).astype(bf16)
        return 0

    for c in first_sides:
        c.wait_recv()
    shifted(xh, 2, 18, 0, rim(0, False))
    lax.fori_loop(2, 16, conv1, 0, unroll=2)

    for c in first:
        c.wait_recv()

    @pl.when(jnp.logical_not(up))
    def _():
        xh[0:2, 1] = jnp.zeros((2, 96, 256), bf16)

    @pl.when(jnp.logical_not(down))
    def _():
        xh[18:20, 1] = jnp.zeros((2, 96, 256), bf16)

    edge = rim(0, True)
    for h in (0, 1, 18, 19):
        shift_row(xh, h, 0, edge)
    for line in (0, 1, 16, 17):
        conv1(line, 0)

    for t in range(9):
        away = (t // 3 - 1) * 6 + t % 3 - 1
        taps[t * 96 : (t + 1) * 96] = pltpu.roll(edge, (128 - away) % 128, 1).astype(bf16)
    pre = dot(w1[...], taps[...])
    side = jnp.where(off, 0.0, (pre * phi(pre)).astype(bf16).astype(f32))
    shifted(hh, 0, 4, 1, side)

    def conv2(h, _):
        s = (xh[h + 2, 1].astype(f32) + dot(w2[...], window(hh, h))).astype(bf16)
        for k in range(3):
            t2[h, 1536 + k * 96 : 1632 + k * 96] = s
        ds[h + 1, 1] = (dot(lhs[...], t2[h]) * SCALE).astype(bf16)
        return 0

    def conv2_pair(i, _):
        for k in range(2):
            conv2(i * 2 + k, 0)
        for k in range(2):
            shift_row(hh, i * 2 + 4 + k, 1, side)
        return 0

    lax.fori_loop(0, 7, conv2_pair, 0)
    for h in (14, 15):
        conv2(h, 0)
    tile[1] = own_tile(lambda h: ds[h + 1, 1])
    second_sides, second = exchange(1, ds.at[1, 1], ds.at[16, 1], ds.at[0, 1], ds.at[17, 1])

    def wide(read, h):
        return jnp.concatenate([read(h * 4 + k) for k in range(4)], axis=1)

    def grads(h, _):
        gacc[:, :96] += dot_nt(
            wide(lambda k: t2[k, :1632], h), wide(lambda k: t2[k, 1536:1632], h)
        )
        return 0

    def grads_out(h, _):
        v[1152:2016, :96] += dot_nt(wide(lambda k: window(hh, k), h), wide(lambda k: ds[k + 1, 1], h))
        return 0

    lax.fori_loop(0, 4, grads, 0)
    mp = sum(dot(m, p[...]) for m in pieces(gacc[1536:1632, :96]))
    for k in range(12):
        part = slice(k * 128, (k + 1) * 128)
        v[k * 96 : 96 + k * 96] = (mp[:, part] - gacc[part].T[:96]) * SCALE
    sums = {
        name: reduce_rows(
            place_here, v, r, k * 1024, 1024, bufs, sent_sum.at[k], got_sum.at[k], name != "E"
        )
        for k, (name, bufs) in enumerate(
            (
                ("E", (a0, a1, a2, a3, a4, a5, a6)),
                ("M", (b0, b1, b2, b3, b4, b5, b6)),
                ("L", (c0, c1, c2, c3, c4, c5, c6)),
            )
        )
    }
    next(sums["E"])

    for c in second_sides + second:
        c.wait_recv()

    @pl.when(jnp.logical_not(up))
    def _():
        ds[0, 1] = jnp.zeros((96, 256), bf16)

    @pl.when(jnp.logical_not(down))
    def _():
        ds[17, 1] = jnp.zeros((96, 256), bf16)

    edge2 = rim(1, True)
    shifted(ds, 0, 6, 1, edge2)

    def back(h, _):
        def dpre(k):
            return (dot(wb[...], window(ds, k)) * gp[k + 1]).astype(bf16)

        v[2048:2912, :96] += dot_nt(wide(lambda k: window(xh, k + 1), h), wide(dpre, h))
        return 0

    next(sums["E"])
    def back_next(i, _):
        back(i, 0)
        for k in range(4):
            shift_row(ds, i * 4 + 6 + k, 1, edge2)
        return 0

    lax.fori_loop(0, 3, back_next, 0)
    back(3, 0)
    next(sums["L"])
    next(sums["E"])
    lax.fori_loop(0, 2, grads_out, 0)
    next(sums["L"])
    lax.fori_loop(2, 4, grads_out, 0)
    for name in "MEMLEMLMELEMLEM":
        next(sums[name], None)
    for _ in sums["L"]:
        pass
    for name in "EM":
        for _ in sums[name]:
            pass
    for c in first_sides + first + second_sides + second:
        c.wait_send()


def finish(r, gin, gout, gproj):
    for t in range(12):
        gproj[:, t * 128 : (t + 1) * 128] = r[t * 96 : 96 + t * 96]
    for t in range(9):
        gout[t] = r[1152 + t * 96 : 1248 + t * 96, :96]
        gin[t] = r[2048 + t * 96 : 2144 + t * 96, :96]


def gradients(features, teacher, conv_in, conv_out, projector):
    bf16, f32 = jnp.bfloat16, jnp.float32
    vmem = pl.BlockSpec(memory_space=pltpu.VMEM)
    hbm = pl.BlockSpec(memory_space=pltpu.HBM)
    sums = pl.pallas_call(
        main_kernel,
        out_shape=jax.ShapeDtypeStruct((ROWS, 128), f32),
        in_specs=[hbm] * 5,
        out_specs=vmem,
        scratch_shapes=[
            pltpu.VMEM((ROWS, 128), f32),
            pltpu.SemaphoreType.DMA((3, 48)),
            pltpu.SemaphoreType.DMA((3, 48)),
            *reduce_scratch(1024, False),
            *reduce_scratch(1024, True),
            *reduce_scratch(1024, True),
            pltpu.VMEM((96, 16, 256), bf16),
            pltpu.VMEM((9, 96, 96), bf16),
            pltpu.VMEM((9, 96, 96), bf16),
            pltpu.VMEM((96, 1536), bf16),
            pltpu.VMEM((1536, 16, 256), bf16),
            pltpu.VMEM((16, 1824, 256), bf16),
            pltpu.VMEM((20, 3, 96, 256), bf16),
            pltpu.VMEM((18, 3, 96, 256), bf16),
            pltpu.VMEM((18, 96, 256), f32),
            pltpu.VMEM((18, 3, 96, 256), bf16),
            pltpu.VMEM((96, 864), bf16),
            pltpu.VMEM((96, 864), bf16),
            pltpu.VMEM((96, 864), bf16),
            pltpu.VMEM((96, 1824), bf16),
            pltpu.VMEM((1632, 128), f32),
            pltpu.VMEM((864, 128), bf16),
            pltpu.VMEM((2, 128, 128), bf16),
            pltpu.VMEM((2, 8, 128, 128), bf16),
            pltpu.SemaphoreType.DMA((10,)),
            pltpu.SemaphoreType.DMA((2, 10)),
            pltpu.SemaphoreType.DMA((2, 10)),
        ],
        compiler_params=pltpu.CompilerParams(
            collective_id=0, has_side_effects=True, vmem_limit_bytes=62 * 2**20
        ),
    )(features, teacher, conv_in, conv_out, projector)
    return pl.pallas_call(
        finish,
        out_shape=(
            jax.ShapeDtypeStruct((9, 96, 96), f32),
            jax.ShapeDtypeStruct((9, 96, 96), f32),
            jax.ShapeDtypeStruct((96, 1536), f32),
        ),
        in_specs=[vmem],
        out_specs=(vmem, vmem, vmem),
    )(sums)


def solution(mesh):
    in_specs = (P(None, "row", "col"), P(None, "row", "col"), P(), P(), P())
    out_specs = (P(), P(), P())
    return jax.shard_map(gradients, mesh=mesh, in_specs=in_specs, out_specs=out_specs, check_vma=False)
```
